512 devices in a mesh: dp: 32 (over z, y_hi), tensor: 16 (over x, y_lo, core).
Axes of the slice: x: 4, y: 8 (y_hi: 4, y_lo: 2; y = y_hi * 2 + y_lo), z: 8, core: 2. Of those that a mesh axis runs over, the one named last changes fastest.
Arguments:
- hidden: bfloat16 [16384, 7168], P('dp', 'tensor'), may hold values from -6 to 6
- w_down: bfloat16 [7168, 576], P('tensor'), may hold values from -0.0625 to 0.0625
- norm_gain: float32 [512], replicated, may hold values from 0.25 to 1.75
- w_up: bfloat16 [512, 32768], P('dp', 'tensor'), may hold values from -0.25 to 0.25
- kv_grad: bfloat16 [16384, 32768], P('dp', 'tensor'), may hold values from -6 to 6
- rope_grad: bfloat16 [16384, 64], P('dp'), may hold values from -6 to 6
Outputs:
- hidden_grad: bfloat16 [16384, 7168], P('dp', 'tensor')
- down_grad: bfloat16 [7168, 576], P('tensor')
- gain_grad: float32 [512], replicated
- up_grad: bfloat16 [512, 32768], P('dp', 'tensor')
The draws below stay inside these ranges and needn't reach their ends.
All inputs are finite; a program needn't handle non-finite values.
Results may differ from the reference program's by a relative error of at most 0.005.
Values may be sent and summed in bfloat16 or wider, within the bound.
No kernel may reach another device: no remote copies, remote signals or barrier semaphores. Data moves between devices by JAX's collectives and lax.ppermute only.
A program may use at most 64 MiB of HBM per device.

```python
import jax
import jax.numpy as jnp
from jax import lax

D = 7168
LAT = 512
ROPE = 64
MB = 256
MICROS = 2
TOKENS = 16384
KVW = 32768
N_DP = 32


def block_levels(stream_key, shape, split, low, high):
    gain = 1.0
    for position, shards_of in split:
        draws = jax.random.uniform(jax.random.fold_in(jax.random.fold_in(stream_key, 6), position), (shards_of,), jnp.float32, low / len(split), high / len(split))
        gain = gain * jnp.repeat(jnp.exp(draws), shape[position] // shards_of).reshape((-1,) + (1,) * (len(shape) - 1 - position))
    return gain


def bell_draw(own_key, shape, deviation, reach, pieces=(), kind=jnp.bfloat16):
    loudness = block_levels(own_key, shape, pieces, -0.22, 0.18) if pieces else 1.0
    values = jax.random.normal(own_key, shape, jnp.float32) * deviation * loudness
    return jnp.minimum(jnp.maximum(values, -reach), reach).astype(kind)


def setup_inputs(seed: int = 0) -> dict:
    seeds = jax.random.split(jax.random.key(seed), 7)
    hidden = bell_draw(seeds[0], (TOKENS, D), 1.0, 6.0, ((0, 32), (1, 16)))
    w_down = bell_draw(seeds[1], (D, LAT + ROPE), D ** -0.5, 0.0625, ((0, 16),))
    norm_gain = jnp.clip(1.0 + 0.15 * jax.random.normal(seeds[2], (LAT,), jnp.float32), 0.25, 1.75)
    w_up = bell_draw(seeds[3], (LAT, KVW), LAT ** -0.5, 0.25, ((0, 32), (1, 16)))
    kv_grad = bell_draw(seeds[4], (TOKENS, KVW), 1.0, 6.0, ((0, 32), (1, 16)))
    rope_grad = bell_draw(seeds[5], (TOKENS, ROPE), 1.0, 6.0, ((0, 32),))
    return {"hidden": hidden, "w_down": w_down, "norm_gain": norm_gain, "w_up": w_up, "kv_grad": kv_grad, "rope_grad": rope_grad}


def reference(hidden, w_down, norm_gain, w_up, kv_grad, rope_grad):
    lat_width = norm_gain.shape[0]
    projected = jnp.dot(hidden, w_down[:, :lat_width], preferred_element_type=jnp.float32)
    inv_rms = lax.rsqrt(lax.optimization_barrier(jnp.mean(projected * projected, axis=1, keepdims=True)) + 1e-06)
    latent = (projected * inv_rms * norm_gain).astype(jnp.bfloat16)
    latent_grad = lax.dot_general(kv_grad, w_up, (((1,), (1,)), ((), ())), preferred_element_type=jnp.float32)
    gain_grad = lax.optimization_barrier(jnp.sum(latent_grad * projected * inv_rms, axis=0))
    scaled = norm_gain * latent_grad
    proj_grad = (inv_rms * scaled - projected * inv_rms * inv_rms * inv_rms * lax.optimization_barrier(jnp.sum(scaled * projected, axis=1, keepdims=True)) / lat_width).astype(jnp.bfloat16)
    joint_grad = jnp.concatenate([proj_grad, rope_grad], axis=1)
    down_grad = lax.dot_general(hidden, joint_grad, (((0,), (0,)), ((), ())), preferred_element_type=jnp.float32).astype(jnp.bfloat16)
    hidden_grad = lax.dot_general(joint_grad, w_down, (((1,), (1,)), ((), ())), preferred_element_type=jnp.float32).astype(jnp.bfloat16)
    group_rows = MICROS * MB

    def add_group(group_index, running):
        first_row = (group_index * group_rows).astype(jnp.int32)
        lat_block = lax.dynamic_slice_in_dim(latent, first_row, group_rows, 0)
        cot_block = lax.dynamic_slice_in_dim(kv_grad, first_row, group_rows, 0)
        group_part = lax.dot_general(lat_block, cot_block, (((0,), (0,)), ((), ())), preferred_element_type=jnp.float32)
        return running + group_part
    running = lax.fori_loop(jnp.int32(0), jnp.int32(N_DP), add_group, jnp.zeros((lat_width, kv_grad.shape[1]), jnp.float32))
    up_grad = running.astype(jnp.bfloat16)
    return (hidden_grad, down_grad, gain_grad, up_grad)
```

```python
import jax
import jax.numpy as jnp
from jax import lax
from jax.sharding import Mesh
from jax.sharding import PartitionSpec as P

ALL = ("z", "yh", "x", "yl", "core")
DP = ("z", "yh")
TENSOR = ("x", "yl", "core")
GAIN_ROWS = 8
LANES = 512


def dot(a, b, dims):
    return lax.dot_general(a, b, (dims, ((), ())), preferred_element_type=jnp.float32)


def two_halves(value):
    high = value.astype(jnp.bfloat16)
    low = (value - high.astype(jnp.float32)).astype(jnp.bfloat16)
    return (high, low)


def scatter_sum(partial, axes, parts):
    pieces = partial.reshape((parts, -1) + partial.shape[1:])
    arrived = lax.all_to_all(pieces, axes, 0, 0, tiled=True)
    return jnp.sum(arrived.astype(jnp.float32), axis=0)


def spread(piece, axes, parts):
    copies = jnp.broadcast_to(piece[None], (parts,) + piece.shape)
    return lax.all_to_all(copies, axes, 0, 0, tiled=True)


def after(value, earlier):
    return lax.optimization_barrier((value, earlier))[0]


def with_gain(down, gain):
    high, low = two_halves(gain)
    lanes = jnp.stack([high, low], axis=-2)
    rows = [(0, 0)] * (lanes.ndim - 2) + [(0, down.shape[-2] - 2), (0, 0)]
    return jnp.concatenate([down.astype(jnp.bfloat16), jnp.pad(lanes, rows)], axis=-1)


def parted(both, width):
    lanes = both[..., :2, width:].astype(jnp.float32)
    return both[..., :width], lanes[..., 0, :] + lanes[..., 1, :]


def body(sizes, hidden, w_down, norm_gain, w_up, kv_grad, rope_grad):
    n_z, n_yh, n_t = sizes
    lat = norm_gain.shape[0]
    width = w_down.shape[1]
    w_up_near = spread(w_up, "yh", n_yh).reshape(-1, w_up.shape[1])
    w_up_all = lax.all_gather(w_up_near, "z", axis=0, tiled=True)

    projected = scatter_sum(
        dot(hidden, w_down[:, :lat], ((1,), (0,))), TENSOR, n_t
    )
    inv_rms = lax.rsqrt(jnp.mean(projected * projected, axis=1, keepdims=True) + 1e-06)
    latent = (projected * inv_rms * norm_gain).astype(jnp.bfloat16)
    latent_all = spread(latent, TENSOR, n_t).reshape(-1, lat)

    up_part = dot(latent_all, kv_grad, ((0,), (0,))).astype(jnp.bfloat16)
    up_sum = lax.psum_scatter(up_part, "z", scatter_dimension=0, tiled=True)
    grad_part = dot(kv_grad, after(w_up_all, up_part), ((1,), (1,)))
    latent_grad = scatter_sum(grad_part.astype(jnp.bfloat16), TENSOR, n_t)
    gain_share = jnp.sum(latent_grad * projected * inv_rms, axis=0)
    scaled = norm_gain * latent_grad
    proj_grad = (
        inv_rms * scaled
        - projected
        * inv_rms
        * inv_rms
        * inv_rms
        * jnp.sum(scaled * projected, axis=1, keepdims=True)
        / lat
    ).astype(jnp.bfloat16)
    high, low = two_halves(gain_share)
    fill = jnp.zeros((GAIN_ROWS - 2, lat), jnp.bfloat16)
    joined = spread(
        jnp.concatenate([proj_grad, high[None], low[None], fill], axis=0), TENSOR, n_t
    )
    rows = proj_grad.shape[0]
    joint_grad = jnp.concatenate([joined[:, :rows].reshape(-1, lat), rope_grad], axis=1)
    gain_group = jnp.sum(joined[:, rows : rows + 2].astype(jnp.float32), axis=(0, 1))

    hidden_grad = dot(joint_grad, w_down, ((1,), (1,))).astype(jnp.bfloat16)

    down_part = dot(hidden, joint_grad, ((0,), (0,)))
    packed = with_gain(down_part.reshape(n_z, -1, width), gain_group.reshape(n_z, -1))
    arrived = lax.all_to_all(packed, "z", 0, 0, tiled=True).astype(jnp.float32)
    down_sum, gain_sum = parted(jnp.sum(arrived, axis=0), width)
    packed = with_gain(down_sum, gain_sum)
    near = packed.shape[0]
    up_rows = up_sum.shape[0] // n_yh
    up_cut = up_sum.reshape(n_yh, up_rows, -1, LANES).transpose(0, 2, 1, 3)
    up_cut = up_cut.reshape(n_yh, -1, LANES)
    up_cut = jnp.pad(up_cut, [(0, 0), (0, 0), (0, packed.shape[1] - LANES)])
    copies = jnp.broadcast_to(packed[None], (n_yh,) + packed.shape)
    both = jnp.concatenate([copies, up_cut], axis=1)
    arrived = lax.all_to_all(both, "yh", 0, 0, tiled=True)
    up_grad = jnp.sum(arrived[:, near:, :LANES].astype(jnp.float32), axis=0)
    up_grad = up_grad.reshape(-1, up_rows, LANES).transpose(1, 0, 2)
    up_grad = up_grad.reshape(up_rows, -1).astype(jnp.bfloat16)
    down_sum, gain_sum = parted(
        jnp.sum(arrived[:, :near].astype(jnp.float32), axis=0), width
    )
    arrived = spread(with_gain(down_sum, gain_sum), "z", n_z)
    down_grad, gain_grad = parted(arrived, width)
    return (hidden_grad, down_grad.reshape(-1, width), gain_grad.reshape(-1), up_grad)


def solution(mesh):
    n_z, n_yh, n_x, n_yl, n_core = 8, 4, 4, 2, 2
    fine = Mesh(mesh.devices.reshape(n_z, n_yh, n_x, n_yl, n_core), ALL)

    def shards(*args):
        return body((n_z, n_yh, n_x * n_yl * n_core), *args)

    return jax.shard_map(
        shards,
        mesh=fine,
        in_specs=(
            P(DP, TENSOR),
            P(TENSOR, None),
            P(),
            P(DP, TENSOR),
            P(DP, TENSOR),
            P(DP, None),
        ),
        out_specs=(P(DP, TENSOR), P(TENSOR, None), P(), P(DP, TENSOR)),
        check_vma=False,
    )
```

```python
import jax
import jax.numpy as jnp
from jax import lax
from jax.sharding import Mesh
from jax.sharding import PartitionSpec as P

ALL = ("z", "yh", "x", "yl", "core")
DP = ("z", "yh")
TENSOR = ("x", "yl", "core")
GAIN_ROWS = 8


def dot(a, b, dims):
    return lax.dot_general(a, b, (dims, ((), ())), preferred_element_type=jnp.float32)


def two_halves(value):
    high = value.astype(jnp.bfloat16)
    low = (value - high.astype(jnp.float32)).astype(jnp.bfloat16)
    return (high, low)


def scatter_sum(partial, axes, parts):
    pieces = partial.reshape((parts, -1) + partial.shape[1:])
    arrived = lax.all_to_all(pieces, axes, 0, 0, tiled=True)
    return jnp.sum(arrived.astype(jnp.float32), axis=0)


def spread(piece, axes, parts):
    copies = jnp.broadcast_to(piece[None], (parts,) + piece.shape)
    return lax.all_to_all(copies, axes, 0, 0, tiled=True)


def shift(value, axis, parts, step):
    return lax.ppermute(value, axis, [(i, (i + step) % parts) for i in range(parts)])


def after(value, earlier):
    return lax.optimization_barrier((value, earlier))[0]


def pack(down, rope, gain):
    high, low = two_halves(gain)
    lanes = jnp.stack([high, low], axis=-2)
    rows = [(0, 0)] * (lanes.ndim - 2) + [(0, rope.shape[-2] - 2), (0, 0)]
    side = jnp.concatenate([rope.astype(jnp.bfloat16), jnp.pad(lanes, rows)], axis=-1)
    return jnp.concatenate([down.astype(jnp.bfloat16), side], axis=-2)


def unpack(packed, near, share):
    lanes = packed[..., near : near + 2, -share:].astype(jnp.float32)
    gain = lanes[..., 0, :] + lanes[..., 1, :]
    return packed[..., :near, :], packed[..., near:, :-share], gain


def body(sizes, hidden, w_down, norm_gain, w_up, kv_grad, rope_grad):
    n_z, n_yh, n_t = sizes
    lat = norm_gain.shape[0]
    here = lax.axis_index("yh")
    blocks = [shift(w_up, "yh", n_yh, k) for k in range(1, n_yh)]
    circle = jnp.concatenate(blocks[::-1] + [w_up] + blocks[::-1], axis=0)
    w_up_near = lax.dynamic_slice_in_dim(
        circle, (n_yh - 1 - here) * w_up.shape[0], n_yh * w_up.shape[0], 0
    )
    w_up_all = lax.all_gather(w_up_near, "z", axis=0, tiled=True)

    projected = scatter_sum(
        dot(hidden, w_down[:, :lat], ((1,), (0,))), TENSOR, n_t
    )
    inv_rms = lax.rsqrt(jnp.mean(projected * projected, axis=1, keepdims=True) + 1e-06)
    latent = (projected * inv_rms * norm_gain).astype(jnp.bfloat16)
    latent_all = spread(latent, TENSOR, n_t).reshape(-1, lat)

    up_part = dot(latent_all, kv_grad, ((0,), (0,))).astype(jnp.bfloat16)
    up_sum = lax.psum_scatter(up_part, "z", scatter_dimension=0, tiled=True)
    grad_part = dot(kv_grad, after(w_up_all, up_part), ((1,), (1,)))
    latent_grad = scatter_sum(grad_part.astype(jnp.bfloat16), TENSOR, n_t)
    gain_share = jnp.sum(latent_grad * projected * inv_rms, axis=0)
    scaled = norm_gain * latent_grad
    proj_grad = (
        inv_rms * scaled
        - projected
        * inv_rms
        * inv_rms
        * inv_rms
        * jnp.sum(scaled * projected, axis=1, keepdims=True)
        / lat
    ).astype(jnp.bfloat16)
    high, low = two_halves(gain_share)
    fill = jnp.zeros((GAIN_ROWS - 2, lat), jnp.bfloat16)
    joined = spread(
        jnp.concatenate([proj_grad, high[None], low[None], fill], axis=0), TENSOR, n_t
    )
    rows = proj_grad.shape[0]
    proj_all = joined[:, :rows].reshape(-1, lat)
    joint_grad = jnp.concatenate([proj_all, rope_grad], axis=1)
    gain_group = jnp.sum(joined[:, rows : rows + 2].astype(jnp.float32), axis=(0, 1))

    hidden_grad = dot(joint_grad, w_down, ((1,), (1,))).astype(jnp.bfloat16)

    down_part = dot(hidden, proj_all, ((0,), (0,))).reshape(n_z, -1, lat)
    rope_part = dot(rope_grad, hidden, ((0,), (0,)))
    near, share = down_part.shape[1], lat // n_z
    packed = pack(
        down_part,
        rope_part.reshape(n_z, -1, rope_part.shape[1]),
        gain_group.reshape(n_z, -1),
    )
    arrived = lax.all_to_all(packed, "z", 0, 0, tiled=True).astype(jnp.float32)
    packed = pack(*unpack(jnp.sum(arrived, axis=0), near, share))
    arrived = spread(after(packed, up_sum), "yh", n_yh).astype(jnp.float32)
    total = jnp.sum(arrived, axis=0)
    up_blocks = after(up_sum.reshape(n_yh, -1, up_sum.shape[1]), total)
    up_grad = lax.dynamic_index_in_dim(up_blocks, here, 0, False).astype(jnp.float32)
    for step in range(1, n_yh):
        block = lax.dynamic_index_in_dim(up_blocks, lax.rem(here + step, n_yh), 0, False)
        up_grad = up_grad + shift(block, "yh", n_yh, step).astype(jnp.float32)
    up_grad = up_grad.astype(jnp.bfloat16)
    arrived = spread(pack(*unpack(total, near, share)), "z", n_z)
    down_grad, rope_down, gain_grad = unpack(arrived, near, share)
    rope_down = rope_down.reshape(-1, rope_down.shape[-1]).T
    down_grad = jnp.concatenate([down_grad.reshape(-1, lat), rope_down], axis=1)
    return (hidden_grad, down_grad, gain_grad.reshape(-1), up_grad)


def solution(mesh):
    n_z, n_yh, n_x, n_yl, n_core = 8, 4, 4, 2, 2
    fine = Mesh(mesh.devices.reshape(n_z, n_yh, n_x, n_yl, n_core), ALL)

    def shards(*args):
        return body((n_z, n_yh, n_x * n_yl * n_core), *args)

    return jax.shard_map(
        shards,
        mesh=fine,
        in_specs=(
            P(DP, TENSOR),
            P(TENSOR, None),
            P(),
            P(DP, TENSOR),
            P(DP, TENSOR),
            P(DP, None),
        ),
        out_specs=(P(DP, TENSOR), P(TENSOR, None), P(), P(DP, TENSOR)),
        check_vma=False,
    )
```

```python
import jax
import jax.numpy as jnp
from jax import lax
from jax.sharding import Mesh
from jax.sharding import PartitionSpec as P

ALL = ("z", "yh", "x", "yl", "core")
DP = ("z", "yh")
TENSOR = ("x", "yl", "core")
GAIN_ROWS = 8


def dot(a, b, dims):
    return lax.dot_general(a, b, (dims, ((), ())), preferred_element_type=jnp.float32)


def two_halves(value):
    high = value.astype(jnp.bfloat16)
    low = (value - high.astype(jnp.float32)).astype(jnp.bfloat16)
    return (high, low)


def scatter_sum(partial, axes, parts):
    pieces = partial.reshape((parts, -1) + partial.shape[1:])
    arrived = lax.all_to_all(pieces, axes, 0, 0, tiled=True)
    return jnp.sum(arrived.astype(jnp.float32), axis=0)


def spread(piece, axes, parts):
    copies = jnp.broadcast_to(piece[None], (parts,) + piece.shape)
    return lax.all_to_all(copies, axes, 0, 0, tiled=True)


def shift(value, axis, parts, step):
    return lax.ppermute(value, axis, [(i, (i + step) % parts) for i in range(parts)])


def after(value, earlier):
    return lax.optimization_barrier((value, earlier))[0]


def pack(down, rope, gain):
    high, low = two_halves(gain)
    lanes = jnp.stack([high, low], axis=-2)
    rows = [(0, 0)] * (lanes.ndim - 2) + [(0, rope.shape[-2] - 2), (0, 0)]
    side = jnp.concatenate([rope.astype(jnp.bfloat16), jnp.pad(lanes, rows)], axis=-1)
    return jnp.concatenate([down.astype(jnp.bfloat16), side], axis=-2)


def unpack(packed, near, share):
    lanes = packed[..., near : near + 2, -share:].astype(jnp.float32)
    gain = lanes[..., 0, :] + lanes[..., 1, :]
    return packed[..., :near, :], packed[..., near:, :-share], gain


def body(sizes, hidden, w_down, norm_gain, w_up, kv_grad, rope_grad):
    n_z, n_yh, n_t = sizes
    lat = norm_gain.shape[0]
    here = lax.axis_index("yh")
    blocks = [shift(w_up, "yh", n_yh, k) for k in range(1, n_yh)]
    circle = jnp.concatenate(blocks[::-1] + [w_up] + blocks[::-1], axis=0)
    w_up_near = lax.dynamic_slice_in_dim(
        circle, (n_yh - 1 - here) * w_up.shape[0], n_yh * w_up.shape[0], 0
    )
    w_up_all = lax.all_gather(w_up_near, "z", axis=0, tiled=True)

    projected = scatter_sum(
        dot(hidden, w_down[:, :lat], ((1,), (0,))), TENSOR, n_t
    )
    inv_rms = lax.rsqrt(jnp.mean(projected * projected, axis=1, keepdims=True) + 1e-06)
    latent = (projected * inv_rms * norm_gain).astype(jnp.bfloat16)
    latent_all = spread(latent, TENSOR, n_t).reshape(-1, lat)

    up_part = dot(latent_all, kv_grad, ((0,), (0,))).astype(jnp.bfloat16)
    up_sum = lax.psum_scatter(up_part, "z", scatter_dimension=0, tiled=True)
    grad_part = dot(kv_grad, after(w_up_all, latent_all), ((1,), (1,)))
    latent_grad = scatter_sum(grad_part.astype(jnp.bfloat16), TENSOR, n_t)
    gain_share = jnp.sum(latent_grad * projected * inv_rms, axis=0)
    scaled = norm_gain * latent_grad
    proj_grad = (
        inv_rms * scaled
        - projected
        * inv_rms
        * inv_rms
        * inv_rms
        * jnp.sum(scaled * projected, axis=1, keepdims=True)
        / lat
    ).astype(jnp.bfloat16)
    high, low = two_halves(gain_share)
    fill = jnp.zeros((GAIN_ROWS - 2, lat), jnp.bfloat16)
    joined = spread(
        jnp.concatenate([proj_grad, high[None], low[None], fill], axis=0), TENSOR, n_t
    )
    rows = proj_grad.shape[0]
    proj_all = joined[:, :rows].reshape(-1, lat)
    joint_grad = jnp.concatenate([proj_all, rope_grad], axis=1)
    gain_group = jnp.sum(joined[:, rows : rows + 2].astype(jnp.float32), axis=(0, 1))

    hidden_grad = dot(joint_grad, w_down, ((1,), (1,))).astype(jnp.bfloat16)

    down_part = dot(hidden, proj_all, ((0,), (0,))).reshape(n_z, -1, lat)
    rope_part = dot(rope_grad, hidden, ((0,), (0,)))
    near, share = down_part.shape[1], lat // n_z
    packed = pack(
        down_part,
        rope_part.reshape(n_z, -1, rope_part.shape[1]),
        gain_group.reshape(n_z, -1),
    )
    arrived = lax.all_to_all(packed, "z", 0, 0, tiled=True).astype(jnp.float32)
    near_sum = after(jnp.sum(arrived, axis=0), hidden_grad)
    packed = pack(*unpack(near_sum, near, share))
    arrived = spread(after(packed, up_sum), "yh", n_yh).astype(jnp.float32)
    total = jnp.sum(arrived, axis=0)
    up_blocks = after(up_sum.reshape(n_yh, -1, up_sum.shape[1]), total)
    up_grad = lax.dynamic_index_in_dim(up_blocks, here, 0, False).astype(jnp.float32)
    for step in range(1, n_yh):
        block = lax.dynamic_index_in_dim(up_blocks, lax.rem(here + step, n_yh), 0, False)
        up_grad = up_grad + shift(block, "yh", n_yh, step).astype(jnp.float32)
    up_grad = up_grad.astype(jnp.bfloat16)
    arrived = spread(pack(*unpack(total, near, share)), "z", n_z)
    down_grad, rope_down, gain_grad = unpack(arrived, near, share)
    rope_down = rope_down.reshape(-1, rope_down.shape[-1]).T
    down_grad = jnp.concatenate([down_grad.reshape(-1, lat), rope_down], axis=1)
    return (hidden_grad, down_grad, gain_grad.reshape(-1), up_grad)


def solution(mesh):
    n_z, n_yh, n_x, n_yl, n_core = 8, 4, 4, 2, 2
    fine = Mesh(mesh.devices.reshape(n_z, n_yh, n_x, n_yl, n_core), ALL)

    def shards(*args):
        return body((n_z, n_yh, n_x * n_yl * n_core), *args)

    return jax.shard_map(
        shards,
        mesh=fine,
        in_specs=(
            P(DP, TENSOR),
            P(TENSOR, None),
            P(),
            P(DP, TENSOR),
            P(DP, TENSOR),
            P(DP, None),
        ),
        out_specs=(P(DP, TENSOR), P(TENSOR, None), P(), P(DP, TENSOR)),
        check_vma=False,
    )
```

```python
import jax
import jax.numpy as jnp
from jax import lax
from jax.sharding import Mesh
from jax.sharding import PartitionSpec as P

ALL = ("z", "yh", "x", "yl", "core")
DP = ("z", "yh")
TENSOR = ("x", "yl", "core")
GAIN_ROWS = 8


def dot(a, b, dims):
    return lax.dot_general(a, b, (dims, ((), ())), preferred_element_type=jnp.float32)


def two_halves(value):
    high = value.astype(jnp.bfloat16)
    low = (value - high.astype(jnp.float32)).astype(jnp.bfloat16)
    return (high, low)


def scatter_sum(partial, axes, parts):
    pieces = partial.reshape((parts, -1) + partial.shape[1:])
    arrived = lax.all_to_all(pieces, axes, 0, 0, tiled=True)
    return jnp.sum(arrived.astype(jnp.float32), axis=0)


def spread(piece, axes, parts):
    copies = jnp.broadcast_to(piece[None], (parts,) + piece.shape)
    return lax.all_to_all(copies, axes, 0, 0, tiled=True)


def shift(value, axis, parts, step):
    return lax.ppermute(value, axis, [(i, (i + step) % parts) for i in range(parts)])


def after(value, earlier):
    return lax.optimization_barrier((value, earlier))[0]


def pack(down, rope, gain):
    high, low = two_halves(gain)
    lanes = jnp.stack([high, low], axis=-2)
    rows = [(0, 0)] * (lanes.ndim - 2) + [(0, rope.shape[-2] - 2), (0, 0)]
    side = jnp.concatenate([rope.astype(jnp.bfloat16), jnp.pad(lanes, rows)], axis=-1)
    return jnp.concatenate([down.astype(jnp.bfloat16), side], axis=-2)


def unpack(packed, near, share):
    lanes = packed[..., near : near + 2, -share:].astype(jnp.float32)
    gain = lanes[..., 0, :] + lanes[..., 1, :]
    return packed[..., :near, :], packed[..., near:, :-share], gain


def body(sizes, hidden, w_down, norm_gain, w_up, kv_grad, rope_grad):
    n_z, n_yh, n_t = sizes
    lat = norm_gain.shape[0]
    here = lax.axis_index("yh")
    w_up_near = lax.all_gather(w_up, "yh", axis=0, tiled=True)
    w_up_all = lax.all_gather(w_up_near, "z", axis=0, tiled=True)

    projected = scatter_sum(
        dot(hidden, w_down[:, :lat], ((1,), (0,))), TENSOR, n_t
    )
    inv_rms = lax.rsqrt(jnp.mean(projected * projected, axis=1, keepdims=True) + 1e-06)
    latent = (projected * inv_rms * norm_gain).astype(jnp.bfloat16)
    latent_all = spread(latent, TENSOR, n_t).reshape(-1, lat)

    up_part = dot(latent_all, kv_grad, ((0,), (0,))).astype(jnp.bfloat16)
    up_sum = lax.psum_scatter(up_part, "z", scatter_dimension=0, tiled=True)
    grad_part = dot(kv_grad, after(w_up_all, latent_all), ((1,), (1,)))
    latent_grad = scatter_sum(grad_part.astype(jnp.bfloat16), TENSOR, n_t)
    gain_share = jnp.sum(latent_grad * projected * inv_rms, axis=0)
    scaled = norm_gain * latent_grad
    proj_grad = (
        inv_rms * scaled
        - projected
        * inv_rms
        * inv_rms
        * inv_rms
        * jnp.sum(scaled * projected, axis=1, keepdims=True)
        / lat
    ).astype(jnp.bfloat16)
    high, low = two_halves(gain_share)
    fill = jnp.zeros((GAIN_ROWS - 2, lat), jnp.bfloat16)
    joined = spread(
        jnp.concatenate([proj_grad, high[None], low[None], fill], axis=0), TENSOR, n_t
    )
    rows = proj_grad.shape[0]
    proj_all = joined[:, :rows].reshape(-1, lat)
    joint_grad = jnp.concatenate([proj_all, rope_grad], axis=1)
    gain_group = jnp.sum(joined[:, rows : rows + 2].astype(jnp.float32), axis=(0, 1))

    hidden_grad = dot(joint_grad, w_down, ((1,), (1,))).astype(jnp.bfloat16)

    down_part = dot(hidden, proj_all, ((0,), (0,))).reshape(n_z, -1, lat)
    rope_part = dot(rope_grad, hidden, ((0,), (0,)))
    near, share = down_part.shape[1], lat // n_z
    packed = pack(
        down_part,
        rope_part.reshape(n_z, -1, rope_part.shape[1]),
        gain_group.reshape(n_z, -1),
    )
    arrived = lax.all_to_all(packed, "z", 0, 0, tiled=True).astype(jnp.float32)
    near_sum = after(jnp.sum(arrived, axis=0), hidden_grad)
    packed = pack(*unpack(near_sum, near, share))
    arrived = spread(after(packed, up_sum), "yh", n_yh).astype(jnp.float32)
    total = jnp.sum(arrived, axis=0)
    up_blocks = after(up_sum.reshape(n_yh, -1, up_sum.shape[1]), total)
    up_grad = lax.dynamic_index_in_dim(up_blocks, here, 0, False).astype(jnp.float32)
    for step in range(1, n_yh):
        block = lax.dynamic_index_in_dim(up_blocks, lax.rem(here + step, n_yh), 0, False)
        up_grad = up_grad + shift(block, "yh", n_yh, step).astype(jnp.float32)
    up_grad = up_grad.astype(jnp.bfloat16)
    arrived = spread(pack(*unpack(total, near, share)), "z", n_z)
    down_grad, rope_down, gain_grad = unpack(arrived, near, share)
    rope_down = rope_down.reshape(-1, rope_down.shape[-1]).T
    down_grad = jnp.concatenate([down_grad.reshape(-1, lat), rope_down], axis=1)
    return (hidden_grad, down_grad, gain_grad.reshape(-1), up_grad)


def solution(mesh):
    n_z, n_yh, n_x, n_yl, n_core = 8, 4, 4, 2, 2
    fine = Mesh(mesh.devices.reshape(n_z, n_yh, n_x, n_yl, n_core), ALL)

    def shards(*args):
        return body((n_z, n_yh, n_x * n_yl * n_core), *args)

    return jax.shard_map(
        shards,
        mesh=fine,
        in_specs=(
            P(DP, TENSOR),
            P(TENSOR, None),
            P(),
            P(DP, TENSOR),
            P(DP, TENSOR),
            P(DP, None),
        ),
        out_specs=(P(DP, TENSOR), P(TENSOR, None), P(), P(DP, TENSOR)),
        check_vma=False,
    )
```
